32 devices in a mesh: row: 4 (over y, x), col: 8 (over z, core).
Axes of the slice: x: 2, y: 2, z: 4, core: 2. Of those that a mesh axis runs over, the one named last changes fastest.
Arguments:
- hist_corr: float32 [16384, 16384], P('row', 'col'), may hold values from -1 to 1
- hist_resp: float32 [16384, 16384], P('row', 'col'), may hold values from -1 to 1, as said below
- row_corr: float32 [128, 16384], P(None, 'col'), may hold values from -1 to 1
- row_resp: float32 [128, 16384], P(None, 'col'), may hold values from -1 to 1
Outputs:
- final_corr: float32 [128, 16384], P(None, 'col')
- final_resp: float32 [128, 16384], P(None, 'col')
The draws below stay inside these ranges and needn't reach their ends.
Inputs may be any that keep to these rules, and one draw needn't show every extreme that they name: hist_resp[s, u] is 0 where u > s and 1 where u == s.
All inputs are finite; a program needn't handle non-finite values.
Results may differ from the reference program's by a relative error of at most 0.00015.
Values sent between devices are 32-bit elements; how exact they have to be, the bound alone decides.
A program may use at most 128 MiB of HBM per device.

```python
import math
import jax
import jax.numpy as jnp
from jax import lax

HIST = 16384
ROWS = 128
BLOCKS = 4


def draw_hist_corr(key, part):
    base_key = jax.random.fold_in(key, 101)
    rough_part = jax.random.uniform(base_key, (HIST, HIST), jnp.float32, -1.0, 1.0)
    return rough_part


def draw_hist_resp(key, part):
    base_key = jax.random.fold_in(key, 202)
    rough_part = jax.random.uniform(base_key, (HIST, HIST), jnp.float32, -1.0, 1.0)
    time_index = jnp.arange(HIST, dtype=jnp.int32)
    later_mask = time_index[:, None] > time_index[None, :]
    diagonal_mask = time_index[:, None] == time_index[None, :]
    filled = jnp.where(diagonal_mask, jnp.float32(1.0), jnp.float32(0.0))
    return jnp.where(later_mask, rough_part, filled).astype(jnp.float32)


def draw_rows(key, salt_value):
    base_key = jax.random.fold_in(key, salt_value)
    time_grid = jnp.arange(HIST, dtype=jnp.int32).astype(jnp.float32) / HIST
    rough_part = jax.random.uniform(base_key, (ROWS, HIST), jnp.float32, -1.0, 1.0)
    return rough_part * (0.55 + 0.45 * time_grid)[None, :]


def draw_row_corr(key, part):
    return draw_rows(key, 303)


def draw_row_resp(key, part):
    return draw_rows(key, 404)


def setup_inputs(seed: int = 0) -> dict:
    splits = jax.random.split(jax.random.key(seed), 5)
    hist_corr = draw_hist_corr(jax.random.fold_in(splits[4], 71), 0)
    hist_resp = draw_hist_resp(jax.random.fold_in(splits[4], 71), 0)
    row_corr = draw_row_corr(jax.random.fold_in(splits[4], 71), 0)
    row_resp = draw_row_resp(jax.random.fold_in(splits[4], 71), 0)
    return {"hist_corr": hist_corr, "hist_resp": hist_resp, "row_corr": row_corr, "row_resp": row_resp}


step_size = 0.2
heat_reservoir_warmth = 0.6

def reference(hist_corr, hist_resp, row_corr, row_resp):
    highest = lax.Precision.HIGHEST
    integration_coefficient = 1.0 / math.sqrt(HIST)
    autocovariance_curve = row_corr
    perturbation_reaction = row_resp
    for block_index in range(BLOCKS):
        history_integrand = 3.0 * autocovariance_curve * perturbation_reaction
        slope_contribution = 1.5 * autocovariance_curve * autocovariance_curve
        norm_enforcing_scalar = heat_reservoir_warmth + integration_coefficient * lax.optimization_barrier(jnp.sum(history_integrand * autocovariance_curve + slope_contribution * perturbation_reaction, axis=1, keepdims=True))
        memory_corr = jnp.dot(history_integrand, hist_corr, precision=highest, preferred_element_type=jnp.float32)
        memory_resp = jnp.dot(history_integrand, hist_resp, precision=highest, preferred_element_type=jnp.float32)
        memory_cross = lax.dot_general(slope_contribution, hist_resp, (((1,), (1,)), ((), ())), precision=highest, preferred_element_type=jnp.float32)
        next_corr = autocovariance_curve + step_size * (integration_coefficient * (memory_corr + memory_cross) - norm_enforcing_scalar * autocovariance_curve)
        next_resp = perturbation_reaction + step_size * (integration_coefficient * memory_resp - norm_enforcing_scalar * perturbation_reaction)
        autocovariance_curve = next_corr
        perturbation_reaction = next_resp
    return (autocovariance_curve, perturbation_reaction)
```

```python
import functools
import math

import jax
import jax.numpy as jnp
from jax import lax
from jax.experimental import pallas as pl
from jax.experimental.pallas import tpu as pltpu
from jax.sharding import PartitionSpec as P

BLOCKS = 4
STEP = 0.2
WARMTH = 0.6


def plain_body(hist_corr, hist_resp, row_corr, row_resp):
    rows = lax.axis_size("row")
    span = row_corr.shape[0] // rows
    coef = 1.0 / math.sqrt(hist_corr.shape[0] * rows)
    start = lax.axis_index("row") * span
    corr = lax.dynamic_slice_in_dim(row_corr, start, span, 0)
    resp = lax.dynamic_slice_in_dim(row_resp, start, span, 0)

    def dot(a, b, dims):
        return lax.dot_general(
            a, b, (dims, ((), ())), precision=lax.Precision.HIGH, preferred_element_type=jnp.float32
        )

    for _ in range(BLOCKS):
        energy = 3.0 * corr * resp
        slope = 1.5 * corr * corr
        mult = lax.psum(jnp.sum(energy * corr + slope * resp, axis=1), "col")
        full = lax.all_gather(corr, "row", axis=0, tiled=True)
        wide = lax.all_gather(energy, "col", axis=1, tiled=True)
        energy_rows = lax.all_to_all(wide, "row", split_axis=1, concat_axis=0, tiled=True)
        part_cross = dot(1.5 * full * full, hist_resp, ((1,), (1,)))
        turned = lax.all_to_all(part_cross, "row", split_axis=0, concat_axis=1, tiled=True)
        cross = lax.psum_scatter(turned, "col", scatter_dimension=1, tiled=True)
        part_corr = dot(energy_rows, hist_corr, ((1,), (0,)))
        part_resp = dot(energy_rows, hist_resp, ((1,), (0,)))
        mem_corr = lax.psum_scatter(part_corr, "row", scatter_dimension=0, tiled=True)
        mem_resp = lax.psum_scatter(part_resp, "row", scatter_dimension=0, tiled=True)
        scalar = WARMTH + coef * mult[:, None]
        next_corr = corr + STEP * (coef * (mem_corr + cross) - scalar * corr)
        resp = resp + STEP * (coef * mem_resp - scalar * resp)
        corr = next_corr
    return (
        lax.all_gather(corr, "row", axis=0, tiled=True),
        lax.all_gather(resp, "row", axis=0, tiled=True),
    )


MESH = pl.DeviceIdType.MESH
F32 = jnp.float32


BF16 = jnp.bfloat16
F8 = jnp.float8_e4m3fn
SCALE = 131072.0
STAGES = 4
PIECE = 128
CH = 512
NN = (((1,), (0,)), ((), ()))
NT = (((1,), (1,)), ((), ()))


def split(x):
    hi = x.astype(BF16)
    return hi, (x - hi.astype(F32)).astype(BF16)


def dot(a, b, dims):
    return lax.dot_general(a, b, dims, preferred_element_type=F32)


def blocks_kernel(coef, R, Z, hc, hr, c0, r0, c_full, r_full, lo_hbm, *refs):
    refs = list(refs)
    take = lambda n: [refs.pop(0) for _ in range(n)]
    hchi, hrhi, hrlo, ring, stage = take(5)
    c_st, r_st, racc, dstack, estack, W = take(6)
    xown, xbuf, up, eall, mrecv, mbuf = take(6)
    bar, isem, ssem, lsem, osem = take(5)
    xs, xr, us, ur, ms, mrs, cs, crs = take(8)
    eus, eur, eds, edr, eis, eir, ps, pr, mus, mur = take(10)
    assert not refs
    T, U = c_st.shape
    M = R * T
    N = 2 * Z
    S = hc.shape[0]
    per = U // CH
    K = S // 4
    r, c = lax.axis_index("row"), lax.axis_index("col")
    z = lax.div(c, 2)
    k = c - 2 * z
    partner = 2 * z + 1 - k
    rows = [lax.rem(r + d, R) for d in range(1, R)]
    cols = [lax.rem(c + d, N) for d in range(1, N)]
    low = z <= r

    def rc(src, dst, ss, rs, row, col):
        return pltpu.make_async_remote_copy(
            src_ref=src, dst_ref=dst, send_sem=ss, recv_sem=rs, device_id=(row, col), device_id_type=MESH
        )

    def at_row(q):
        return pl.ds(pl.multiple_of(q * T, T), T)

    def half(h):
        return pl.ds(pl.multiple_of(h * U, U), U)

    def chunk(i, base=0):
        return pl.ds(base + i * CH, CH)

    pieces = S // PIECE
    group = CH // PIECE

    def x_row(t):
        side = jnp.where(lax.rem(t, 2) == 0, 1 - k, k)
        return side * U + lax.div(t, 2) * CH

    def piece_row(n):
        return pl.multiple_of(x_row(lax.div(n, group)) + lax.rem(n, group) * PIECE, PIECE)

    def piece_copy(src, start, n):
        slot = lax.rem(n, STAGES)
        return pltpu.make_async_copy(src.at[pl.ds(start, PIECE)], stage.at[slot], ssem.at[slot])

    def piece_start(n):
        @pl.when(n < pieces)
        def _():
            piece_copy(hr, piece_row(n), n).start()

        @pl.when(jnp.logical_and(n >= pieces, n < 2 * pieces))
        def _():
            piece_copy(hc, pl.multiple_of((n - pieces) * PIECE, PIECE), n).start()

    def piece_split(n, hi_ref, row, lo_ref, lo_row):
        slot = lax.rem(n, STAGES)
        piece_copy(hc, 0, n).wait()

        @pl.loop(0, PIECE // 32)
        def _(i):
            x = stage[slot, pl.ds(pl.multiple_of(i * 32, 32), 32), :]
            hi = x.astype(BF16)
            hi_ref[pl.ds(pl.multiple_of(row + i * 32, 32), 32), :] = hi
            lo_ref[pl.ds(pl.multiple_of(lo_row + i * 32, 32), 32), :] = ((x - hi.astype(F32)) * SCALE).astype(F8)

        piece_start(n + STAGES)

    for n in range(STAGES):
        piece_start(jnp.int32(n))
    inits = [
        pltpu.make_async_copy(c0, c_full, isem.at[0]),
        pltpu.make_async_copy(c0.at[at_row(r)], c_st, isem.at[1]),
        pltpu.make_async_copy(r0.at[at_row(r)], r_st, isem.at[2]),
    ]
    for cp in inits:
        cp.start()
    barrier = pltpu.get_barrier_semaphore()

    def greet(sem):
        for q in rows:
            pl.semaphore_signal(sem, inc=1, device_id=(q, c), device_id_type=MESH)
        for q in cols:
            pl.semaphore_signal(sem, inc=1, device_id=(r, q), device_id_type=MESH)

    greet(barrier)
    for cp in inits:
        cp.wait()
    pl.semaphore_wait(barrier, R - 1 + N - 1)

    def flow(p, step):
        ss, rs = (eus, eur) if step > 0 else (eds, edr)
        return rc(eall.at[p], eall.at[p], ss.at[p], rs.at[p], r, c + step)

    def inplane(d, p):
        return rc(eall.at[p], W.at[at_row(r), half(k)], eis.at[d], eir.at[d], p, c)

    def turn(p):
        @pl.when(p == r)
        def _():
            W[at_row(r), half(k)] = eall[p]

        @pl.when(p != r)
        def _():
            inplane(lax.rem(p - r + R, R) - 1, p).start()

    pair = rc(W.at[:, half(k)], W.at[:, half(k)], ps, pr, r, partner)

    def share(h):
        @pl.when(jnp.logical_or(z - r == h, r - z == h))
        def _():
            for d in range(R - 1):
                inplane(d, rows[d]).wait_recv()
            pair.start()

    def hop(h):
        @pl.when(z - h >= 0)
        def _():
            flow(z - h, 2).wait_recv()

            @pl.when(z < Z - 1)
            def _():
                flow(z - h, 2).start()

        @pl.when(z + h <= Z - 1)
        def _():
            flow(z + h, -2).wait_recv()

            @pl.when(z > 0)
            def _():
                flow(z + h, -2).start()

            turn(z + h)

        @pl.when(z - h >= 0)
        def _():
            turn(z - h)

        share(h - 1)

    def mucopy(d):
        return rc(mbuf.at[c], mbuf.at[c], mus.at[d], mur.at[d], r, cols[d])

    def xcopy(i):
        return rc(c_full.at[:, chunk(i)], xbuf.at[:, chunk(i)], xs.at[i], xr.at[i], r, partner)

    def upcopy(i, col):
        return rc(xown.at[:, chunk(i)], up.at[:, chunk(i)], us.at[i], ur.at[i], r, col)

    def mcopy(d, which, i):
        q = rows[d]
        return rc(
            W.at[at_row(q), chunk(i, which * U)],
            mrecv.at[d, which, :, chunk(i)],
            ms.at[d, which, i],
            mrs.at[d, which, i],
            q,
            c,
        )

    def gcopy(d, which):
        src, dst = (c_st, c_full) if which == 0 else (r_st, r_full)
        return rc(src, dst.at[at_row(r)], cs.at[d, which], crs.at[d, which], rows[d], c)

    def climb(zz, i):
        @pl.when(jnp.logical_and(z == zz, low))
        def _():
            xcopy(i).wait()
            both = xown[:, chunk(i)] + xbuf[:, chunk(i)]
            if zz > 0:
                upcopy(i, c).wait_recv()
                both = both + up[:, chunk(i)]
            xown[:, chunk(i)] = both
            if zz < Z - 1:
                @pl.when(z < r)
                def _():
                    upcopy(i, c + 2).start()

    def stack(dst_ref, i, x):
        hi, lo = split(x)
        dst_ref[pl.ds(pl.multiple_of(i * 32, 32), 32), :] = hi
        dst_ref[pl.ds(pl.multiple_of(M + i * 32, 32), 32), :] = lo

    def e_ready():
        share(Z - 1)
        pair.wait()

        @pl.loop(0, M // 32)
        def _(i):
            stack(estack, i, W[pl.ds(pl.multiple_of(i * 32, 32), 32), :])

    def x_tile(b, t):
        @pl.when(b == 0)
        def _():
            @pl.loop(0, group)
            def _(g):
                n = t * group + g
                row = piece_row(n)
                piece_split(n, hrhi, row, hrlo, row)

        @pl.when(low)
        def _():
            out = c_full if t % 2 == 0 else xown
            where = chunk(t // 2)
            start = pl.multiple_of(x_row(jnp.int32(t)), CH)
            out[:, where] = jnp.zeros((M, CH), F32)

            @pl.loop(0, per)
            def _(j):
                at = pl.ds(pl.multiple_of(j * CH, CH), CH)
                both = dstack[:, at]
                p = dot(both, hrhi[pl.ds(start, CH), at], NT)
                q = dot(both[:M], hrlo[pl.ds(start, CH), at].astype(BF16), NT)
                out[:, where] += p[:M] + p[M:] + q * (1.0 / SCALE)

            if t % 2 == 0:
                xcopy(t // 2).start()

    def resp_tile(i):
        @pl.when(low)
        def _():
            where = chunk(i, U)
            W[:, where] = jnp.zeros((M, CH), F32)

            @pl.loop(0, S // CH)
            def _(j):
                at = pl.ds(pl.multiple_of(j * CH, CH), CH)
                both = estack[:, at]
                p = dot(both, hrhi[at, chunk(i)], NN)
                q = dot(both[:M], hrlo[at, chunk(i)].astype(BF16), NN)
                W[:, where] += p[:M] + p[M:] + q * (1.0 / SCALE)

            for d in range(R - 1):
                mcopy(d, 1, i).start()

    def lo_in(j):
        return pltpu.make_async_copy(lo_hbm.at[pl.ds(j * K, K)], ring.at[j % 2], lsem.at[j % 2])

    def lo_out(j):
        return pltpu.make_async_copy(ring.at[j % 2], lo_hbm.at[pl.ds(j * K, K)], osem.at[j % 2])

    def corr_part(b, j):
        @pl.when(b == 0)
        def _():
            if j >= 2:
                lo_out(j - 2).wait()

            @pl.loop(0, K // PIECE)
            def _(g):
                n = pieces + j * (K // PIECE) + g
                piece_split(n, hchi, j * K + g * PIECE, ring.at[j % 2], g * PIECE)

            lo_out(j).start()

        @pl.when(b > 0)
        def _():
            lo_in(j).wait()

        @pl.loop(0, per)
        def _(i):
            at = pl.ds(pl.multiple_of(i * CH, CH), CH)
            both = estack[:, j * K : (j + 1) * K]
            p = dot(both, hchi[j * K : (j + 1) * K, at], NN)
            q = dot(both[:M], ring[j % 2, :, at].astype(BF16), NN)
            out = p[:M] + p[M:] + q * (1.0 / SCALE)
            if j == 0:
                W[:, at] = out
            else:
                W[:, at] += out

        if j < 2:
            @pl.when(b > 0)
            def _():
                lo_in(j + 2).start()

    @pl.loop(0, BLOCKS)
    def _(b):
        energy = 3.0 * c_st[...] * r_st[...]
        eall[z] = energy
        terms = energy * c_st[...] + 1.5 * c_st[...] * c_st[...] * r_st[...]
        part = terms[:, :128]
        for i in range(1, U // 128):
            part = part + terms[:, i * 128 : (i + 1) * 128]
        mbuf[c] = part

        @pl.when(b > 0)
        def _():
            lo_in(0).start()
            lo_in(1).start()
            pl.semaphore_wait(bar, R - 1 + N - 1)

        @pl.when(z < Z - 1)
        def _():
            flow(z, 2).start()

        @pl.when(z > 0)
        def _():
            flow(z, -2).start()

        turn(z)
        for d in range(N - 1):
            mucopy(d).start()
        hop(1)

        @pl.when(b > 0)
        def _():
            for d in range(R - 1):
                gcopy(d, 0).wait()

        @pl.loop(0, M // 32)
        def _(i):
            old = c_full[pl.ds(pl.multiple_of(i * 32, 32), 32), :]
            stack(dstack, i, 1.5 * old * old)

        hooks = {}

        def hook(n, f, *args):
            hooks.setdefault(n, []).append((f, args))

        hook(1, hop, 2)
        for i in range(per):
            hook(min(2 * i + 2, 7), climb, 0, i)
        hook(6, climb, 1, 0)
        hook(7, hop, 3)
        hook(7, climb, 1, 1)
        hook(7, e_ready)
        for n, zz, i in [(8, 1, 2), (8, 2, 0), (9, 1, 3), (9, 2, 1), (10, 2, 2), (10, 3, 0), (11, 2, 3), (12, 3, 1), (14, 3, 2)]:
            hook(n, climb, zz, i)
        hook(15, climb, 3, 3)
        for n in range(16):
            if n < 8:
                x_tile(b, n)
            elif n < 12:
                resp_tile(n - 8)
            else:
                corr_part(b, n - 12)
            for f, args in hooks.get(n, ()):
                f(*args)

        for i in range(per):
            @pl.when(z == r)
            def _():
                W[:, chunk(i)] += xown[:, chunk(i)]

            for d in range(R - 1):
                mcopy(d, 0, i).start()

        for d in range(N - 1):
            mucopy(d).wait_recv()
        total = mbuf[0]
        for i in range(1, N):
            total = total + mbuf[i]
        scalar = WARMTH + coef * jnp.sum(total, axis=1, keepdims=True)
        racc[...] = jnp.zeros((T, U), F32)

        @pl.when(low)
        def _():
            racc[...] = W[at_row(r), U:]

        for d in range(R - 1):
            @pl.when(z <= lax.rem(r - d - 1 + R, R))
            def _():
                for i in range(per):
                    mcopy(d, 1, i).wait_recv()
                racc[...] += mrecv[d, 1]

        r_st[...] = r_st[...] + STEP * (coef * racc[...] - scalar * r_st[...])

        @pl.when(b == BLOCKS - 1)
        def _():
            r_full[at_row(r), :] = r_st[...]
            for d in range(R - 1):
                gcopy(d, 1).start()

        racc[...] = W[at_row(r), :U]
        for d in range(R - 1):
            for i in range(per):
                mcopy(d, 0, i).wait_recv()
            racc[...] += mrecv[d, 0]
        c_st[...] = c_st[...] + STEP * (coef * racc[...] - scalar * c_st[...])
        c_full[at_row(r), :] = c_st[...]
        for d in range(R - 1):
            gcopy(d, 0).start()

        for d in range(N - 1):
            mucopy(d).wait_send()
        for p in range(Z):
            @pl.when(jnp.logical_and(p <= z, z < Z - 1))
            def _():
                flow(p, 2).wait_send()

            @pl.when(jnp.logical_and(p >= z, z > 0))
            def _():
                flow(p, -2).wait_send()
        for d in range(R - 1):
            inplane(d, rows[d]).wait_send()
            for i in range(per):
                mcopy(d, 0, i).wait_send()

        @pl.when(low)
        def _():
            for d in range(R - 1):
                for i in range(per):
                    mcopy(d, 1, i).wait_send()

        @pl.when(z < r)
        def _():
            for i in range(per):
                upcopy(i, c + 2).wait_send()

        @pl.when(b == 0)
        def _():
            lo_out(2).wait()
            lo_out(3).wait()

        @pl.when(b < BLOCKS - 1)
        def _():
            greet(bar)

    for which in range(2):
        for d in range(R - 1):
            gcopy(d, which).wait()


def kernel_body(hist_corr, hist_resp, row_corr, row_resp):
    R, N = lax.axis_size("row"), lax.axis_size("col")
    Z = N // 2
    M, U = row_corr.shape
    S = hist_corr.shape[0]
    T = M // R
    per = U // CH
    coef = 1.0 / math.sqrt(S * R)
    dma, vmem = pltpu.SemaphoreType.DMA, pltpu.VMEM
    scratch = [
        vmem((S, U), BF16),
        vmem((S, U), BF16),
        vmem((S, U), F8),
        vmem((2, S // 4, U), F8),
        vmem((STAGES, PIECE, U), F32),
        vmem((T, U), F32),
        vmem((T, U), F32),
        vmem((T, U), F32),
        vmem((2 * M, U), BF16),
        vmem((2 * M, 2 * U), BF16),
        vmem((M, 2 * U), F32),
        vmem((M, U), F32),
        vmem((M, U), F32),
        vmem((M, U), F32),
        vmem((Z, T, U), F32),
        vmem((R - 1, 2, T, U), F32),
        vmem((N, T, 128), F32),
        pltpu.SemaphoreType.REGULAR,
        dma((3,)),
        dma((STAGES,)),
        dma((2,)),
        dma((2,)),
    ]
    scratch += [dma((per,))] * 4 + [dma((R - 1, 2, per))] * 2 + [dma((R - 1, 2))] * 2
    scratch += [dma((Z,))] * 4 + [dma((R - 1,))] * 2 + [dma, dma] + [dma((N - 1,))] * 2
    hbm, whole = pl.BlockSpec(memory_space=pl.ANY), pl.BlockSpec(memory_space=pltpu.VMEM)
    full = jax.ShapeDtypeStruct((M, U), F32)
    out = pl.pallas_call(
        functools.partial(blocks_kernel, coef, R, Z),
        out_shape=[full, full, jax.ShapeDtypeStruct((S, U), F8)],
        in_specs=[hbm] * 4,
        out_specs=[whole, whole, hbm],
        scratch_shapes=scratch,
        name="blocks",
        compiler_params=pltpu.CompilerParams(collective_id=1, has_side_effects=True, vmem_limit_bytes=67_043_328),
    )(hist_corr, hist_resp, row_corr, row_resp)
    return tuple(out[:2])


def solution(mesh):
    R, N = mesh.shape["row"], mesh.shape["col"]
    body = kernel_body if N == 2 * R and R == 4 else plain_body
    in_specs = (P("row", "col"), P("row", "col"), P(None, "col"), P(None, "col"))
    out_specs = (P(None, "col"), P(None, "col"))
    return jax.shard_map(body, mesh=mesh, in_specs=in_specs, out_specs=out_specs, check_vma=False)
```

```python
import functools
import math

import jax
import jax.numpy as jnp
from jax import lax
from jax.experimental import pallas as pl
from jax.experimental.pallas import tpu as pltpu
from jax.sharding import PartitionSpec as P

BLOCKS = 4
STEP = 0.2
WARMTH = 0.6


def plain_body(hist_corr, hist_resp, row_corr, row_resp):
    rows = lax.axis_size("row")
    span = row_corr.shape[0] // rows
    coef = 1.0 / math.sqrt(hist_corr.shape[0] * rows)
    start = lax.axis_index("row") * span
    corr = lax.dynamic_slice_in_dim(row_corr, start, span, 0)
    resp = lax.dynamic_slice_in_dim(row_resp, start, span, 0)

    def dot(a, b, dims):
        return lax.dot_general(
            a, b, (dims, ((), ())), precision=lax.Precision.HIGH, preferred_element_type=jnp.float32
        )

    for _ in range(BLOCKS):
        energy = 3.0 * corr * resp
        slope = 1.5 * corr * corr
        mult = lax.psum(jnp.sum(energy * corr + slope * resp, axis=1), "col")
        full = lax.all_gather(corr, "row", axis=0, tiled=True)
        wide = lax.all_gather(energy, "col", axis=1, tiled=True)
        energy_rows = lax.all_to_all(wide, "row", split_axis=1, concat_axis=0, tiled=True)
        part_cross = dot(1.5 * full * full, hist_resp, ((1,), (1,)))
        turned = lax.all_to_all(part_cross, "row", split_axis=0, concat_axis=1, tiled=True)
        cross = lax.psum_scatter(turned, "col", scatter_dimension=1, tiled=True)
        part_corr = dot(energy_rows, hist_corr, ((1,), (0,)))
        part_resp = dot(energy_rows, hist_resp, ((1,), (0,)))
        mem_corr = lax.psum_scatter(part_corr, "row", scatter_dimension=0, tiled=True)
        mem_resp = lax.psum_scatter(part_resp, "row", scatter_dimension=0, tiled=True)
        scalar = WARMTH + coef * mult[:, None]
        next_corr = corr + STEP * (coef * (mem_corr + cross) - scalar * corr)
        resp = resp + STEP * (coef * mem_resp - scalar * resp)
        corr = next_corr
    return (
        lax.all_gather(corr, "row", axis=0, tiled=True),
        lax.all_gather(resp, "row", axis=0, tiled=True),
    )


MESH = pl.DeviceIdType.MESH
F32 = jnp.float32


BF16 = jnp.bfloat16
F8 = jnp.float8_e4m3fn
SCALE = 131072.0
STAGES = 4
PIECE = 128
CH = 512
KX = 1024
NN = (((1,), (0,)), ((), ()))
NT = (((1,), (1,)), ((), ()))


def split(x):
    hi = x.astype(BF16)
    return hi, (x - hi.astype(F32)).astype(BF16)


def dot(a, b, dims):
    return lax.dot_general(a, b, dims, preferred_element_type=F32)


def blocks_kernel(coef, R, Z, hc, hr, c0, r0, c_full, r_full, lo_hbm, *refs):
    refs = list(refs)
    take = lambda n: [refs.pop(0) for _ in range(n)]
    hchi, hrhi, hrlo, ring, stage = take(5)
    c_st, r_st, racc, dstack, estack, W = take(6)
    xown, xbuf, up, eall, mrecv, mbuf = take(6)
    bar, isem, ssem, lsem, osem = take(5)
    xs, xr, us, ur, ms, mrs, cs, crs = take(8)
    eus, eur, eds, edr, eis, eir, ps, pr, mus, mur = take(10)
    assert not refs
    T, U = c_st.shape
    H = T // 2
    M = R * T
    N = 2 * Z
    S = hc.shape[0]
    per = U // CH
    K = S // 4
    r, c = lax.axis_index("row"), lax.axis_index("col")
    z = lax.div(c, 2)
    k = c - 2 * z
    partner = 2 * z + 1 - k
    rows = [lax.rem(r + d, R) for d in range(1, R)]
    cols = [lax.rem(c + d, N) for d in range(1, N)]
    low = z <= r

    def rc(src, dst, ss, rs, row, col):
        return pltpu.make_async_remote_copy(
            src_ref=src, dst_ref=dst, send_sem=ss, recv_sem=rs, device_id=(row, col), device_id_type=MESH
        )

    def at_row(q):
        return pl.ds(pl.multiple_of(q * T, T), T)

    def half(h):
        return pl.ds(pl.multiple_of(h * U, U), U)

    def chunk(i, base=0):
        return pl.ds(base + i * CH, CH)

    pieces = S // PIECE
    group = CH // PIECE

    def x_row(t):
        side = jnp.where(lax.rem(t, 2) == 0, 1 - k, k)
        return side * U + lax.div(t, 2) * CH

    def piece_row(n):
        return pl.multiple_of(x_row(lax.div(n, group)) + lax.rem(n, group) * PIECE, PIECE)

    def piece_copy(src, start, n):
        slot = lax.rem(n, STAGES)
        return pltpu.make_async_copy(src.at[pl.ds(start, PIECE)], stage.at[slot], ssem.at[slot])

    def piece_start(n):
        @pl.when(n < pieces)
        def _():
            piece_copy(hr, piece_row(n), n).start()

        @pl.when(jnp.logical_and(n >= pieces, n < 2 * pieces))
        def _():
            piece_copy(hc, pl.multiple_of((n - pieces) * PIECE, PIECE), n).start()

    def piece_split(n, hi_ref, row, lo_ref, lo_row):
        slot = lax.rem(n, STAGES)
        piece_copy(hc, 0, n).wait()

        @pl.loop(0, PIECE // 32)
        def _(i):
            x = stage[slot, pl.ds(pl.multiple_of(i * 32, 32), 32), :]
            hi = x.astype(BF16)
            hi_ref[pl.ds(pl.multiple_of(row + i * 32, 32), 32), :] = hi
            lo_ref[pl.ds(pl.multiple_of(lo_row + i * 32, 32), 32), :] = ((x - hi.astype(F32)) * SCALE).astype(F8)

        piece_start(n + STAGES)

    for n in range(STAGES):
        piece_start(jnp.int32(n))
    inits = [
        pltpu.make_async_copy(c0, c_full, isem.at[0]),
        pltpu.make_async_copy(c0.at[at_row(r)], c_st, isem.at[1]),
        pltpu.make_async_copy(r0.at[at_row(r)], r_st, isem.at[2]),
    ]
    for cp in inits:
        cp.start()
    barrier = pltpu.get_barrier_semaphore()

    def greet(sem):
        for q in rows:
            pl.semaphore_signal(sem, inc=1, device_id=(q, c), device_id_type=MESH)
        for q in cols:
            pl.semaphore_signal(sem, inc=1, device_id=(r, q), device_id_type=MESH)

    greet(barrier)
    for cp in inits:
        cp.wait()
    pl.semaphore_wait(barrier, R - 1 + N - 1)

    def part(s):
        return pl.ds(s * H, H)

    def e_rows(q, s):
        return pl.ds(pl.multiple_of(q * T + s * H, H), H)

    def flow(p, step, s):
        ss, rs = (eus, eur) if step > 0 else (eds, edr)
        return rc(eall.at[p, part(s)], eall.at[p, part(s)], ss.at[p, s], rs.at[p, s], r, c + step)

    def inplane(d, p, s):
        return rc(eall.at[p, part(s)], W.at[e_rows(r, s), half(k)], eis.at[d, s], eir.at[d, s], p, c)

    def turn(p, s):
        @pl.when(p == r)
        def _():
            W[e_rows(r, s), half(k)] = eall[p, part(s)]

        @pl.when(p != r)
        def _():
            inplane(lax.rem(p - r + R, R) - 1, p, s).start()

    def pair(q):
        piece = W.at[at_row(q), half(k)]
        return rc(piece, piece, ps.at[q], pr.at[q], r, partner)

    def share(h):
        @pl.when(jnp.logical_or(z - r == h, r - z == h))
        def _():
            pair(r).start()
            for d in range(R - 1):
                for s in range(2):
                    inplane(d, rows[d], s).wait_recv()
                pair(lax.rem(r - d - 1 + R, R)).start()

    def hop(h, s):
        @pl.when(z - h >= 0)
        def _():
            flow(z - h, 2, s).wait_recv()

            @pl.when(z < Z - 1)
            def _():
                flow(z - h, 2, s).start()

        @pl.when(z + h <= Z - 1)
        def _():
            flow(z + h, -2, s).wait_recv()

            @pl.when(z > 0)
            def _():
                flow(z + h, -2, s).start()

            turn(z + h, s)

        @pl.when(z - h >= 0)
        def _():
            turn(z - h, s)

    def mucopy(d):
        return rc(mbuf.at[c], mbuf.at[c], mus.at[d], mur.at[d], r, cols[d])

    def xcopy(i):
        return rc(c_full.at[:, chunk(i)], xbuf.at[:, chunk(i)], xs.at[i], xr.at[i], r, partner)

    def upcopy(i, col):
        return rc(xown.at[:, chunk(i)], up.at[:, chunk(i)], us.at[i], ur.at[i], r, col)

    def mcopy(d, which, i):
        q = rows[d]
        return rc(
            W.at[at_row(q), chunk(i, which * U)],
            mrecv.at[d, which, :, chunk(i)],
            ms.at[d, which, i],
            mrs.at[d, which, i],
            q,
            c,
        )

    def gcopy(d, which):
        src, dst = (c_st, c_full) if which == 0 else (r_st, r_full)
        return rc(src, dst.at[at_row(r)], cs.at[d, which], crs.at[d, which], rows[d], c)

    def climb(zz, i):
        @pl.when(jnp.logical_and(z == zz, low))
        def _():
            xcopy(i).wait()
            both = xown[:, chunk(i)] + xbuf[:, chunk(i)]
            if zz > 0:
                upcopy(i, c).wait_recv()
                both = both + up[:, chunk(i)]
            xown[:, chunk(i)] = both
            if zz < Z - 1:
                @pl.when(z < r)
                def _():
                    upcopy(i, c + 2).start()

    def stack(dst_ref, i, x):
        hi, lo = split(x)
        dst_ref[pl.ds(pl.multiple_of(i * 32, 32), 32), :] = hi
        dst_ref[pl.ds(pl.multiple_of(M + i * 32, 32), 32), :] = lo

    def e_ready():
        share(Z - 1)
        for q in range(R):
            pair(q).wait()

        @pl.loop(0, M // 32)
        def _(i):
            stack(estack, i, W[pl.ds(pl.multiple_of(i * 32, 32), 32), :])

    def x_tile(b, t):
        @pl.when(b == 0)
        def _():
            @pl.loop(0, group)
            def _(g):
                n = t * group + g
                row = piece_row(n)
                piece_split(n, hrhi, row, hrlo, row)

        @pl.when(low)
        def _():
            out = c_full if t % 2 == 0 else xown
            where = chunk(t // 2)
            start = pl.multiple_of(x_row(jnp.int32(t)), CH)
            out[:, where] = jnp.zeros((M, CH), F32)

            @pl.loop(0, U // KX)
            def _(j):
                at = pl.ds(pl.multiple_of(j * KX, KX), KX)
                both = dstack[:, at]
                p = dot(both, hrhi[pl.ds(start, CH), at], NT)
                q = dot(both[:M], hrlo[pl.ds(start, CH), at].astype(BF16), NT)
                out[:, where] += p[:M] + p[M:] + q * (1.0 / SCALE)

            if t % 2 == 0:
                xcopy(t // 2).start()

    def resp_tile(i):
        @pl.when(low)
        def _():
            where = chunk(i, U)
            W[:, where] = jnp.zeros((M, CH), F32)

            @pl.loop(0, S // K)
            def _(j):
                at = pl.ds(pl.multiple_of(j * K, K), K)
                both = estack[:, at]
                p = dot(both, hrhi[at, chunk(i)], NN)
                q = dot(both[:M], hrlo[at, chunk(i)].astype(BF16), NN)
                W[:, where] += p[:M] + p[M:] + q * (1.0 / SCALE)

            for d in range(R - 1):
                mcopy(d, 1, i).start()

    def lo_in(j):
        return pltpu.make_async_copy(lo_hbm.at[pl.ds(j * K, K)], ring.at[j % 2], lsem.at[j % 2])

    def lo_out(j):
        return pltpu.make_async_copy(ring.at[j % 2], lo_hbm.at[pl.ds(j * K, K)], osem.at[j % 2])

    def corr_part(b, j):
        @pl.when(b == 0)
        def _():
            if j >= 2:
                lo_out(j - 2).wait()

            @pl.loop(0, K // PIECE)
            def _(g):
                n = pieces + j * (K // PIECE) + g
                piece_split(n, hchi, j * K + g * PIECE, ring.at[j % 2], g * PIECE)

            lo_out(j).start()

        @pl.when(b > 0)
        def _():
            lo_in(j).wait()

        @pl.loop(0, per)
        def _(i):
            at = pl.ds(pl.multiple_of(i * CH, CH), CH)
            both = estack[:, j * K : (j + 1) * K]
            p = dot(both, hchi[j * K : (j + 1) * K, at], NN)
            q = dot(both[:M], ring[j % 2, :, at].astype(BF16), NN)
            out = p[:M] + p[M:] + q * (1.0 / SCALE)
            if j == 0:
                W[:, at] = out
            else:
                W[:, at] += out

        if j < 2:
            @pl.when(b > 0)
            def _():
                lo_in(j + 2).start()

    @pl.loop(0, BLOCKS)
    def _(b):
        energy = 3.0 * c_st[...] * r_st[...]
        eall[z] = energy
        terms = energy * c_st[...] + 1.5 * c_st[...] * c_st[...] * r_st[...]
        part = terms[:, :128]
        for i in range(1, U // 128):
            part = part + terms[:, i * 128 : (i + 1) * 128]
        mbuf[c] = part

        @pl.when(b > 0)
        def _():
            lo_in(0).start()
            lo_in(1).start()
            pl.semaphore_wait(bar, R - 1 + N - 1)

        for s in range(2):
            @pl.when(z < Z - 1)
            def _():
                flow(z, 2, s).start()

            @pl.when(z > 0)
            def _():
                flow(z, -2, s).start()

        for s in range(2):
            turn(z, s)
        for d in range(N - 1):
            mucopy(d).start()
        hop(1, 0)
        hop(1, 1)
        hop(2, 0)

        @pl.when(b > 0)
        def _():
            for d in range(R - 1):
                gcopy(d, 0).wait()

        @pl.loop(0, M // 32)
        def _(i):
            old = c_full[pl.ds(pl.multiple_of(i * 32, 32), 32), :]
            stack(dstack, i, 1.5 * old * old)

        hooks = {}

        def hook(n, f, *args):
            hooks.setdefault(n, []).append((f, args))

        for i in range(per):
            hook(min(2 * i + 2, 7), climb, 0, i)
        hook(1, hop, 3, 1)
        hook(3, share, 0)
        hook(5, share, 1)
        hook(6, share, 2)
        hook(7, climb, 1, 0)
        hook(7, e_ready)
        for n, zz, i in [(8, 1, 1), (9, 2, 0), (11, 1, 2), (11, 2, 1), (12, 3, 0), (14, 1, 3), (14, 2, 2)]:
            hook(n, climb, zz, i)
        hop(2, 1)
        hop(3, 0)
        for n in range(16):
            if n < 8:
                x_tile(b, n)
            elif n < 12:
                resp_tile(n - 8)
            else:
                corr_part(b, n - 12)
            for f, args in hooks.get(n, ()):
                f(*args)

        for i in range(per):
            if i == per - 1:
                climb(Z - 2, i)
            if i >= 1:
                climb(Z - 1, i)

            @pl.when(z == r)
            def _():
                W[:, chunk(i)] += xown[:, chunk(i)]

            for d in range(R - 1):
                mcopy(d, 0, i).start()

        for d in range(N - 1):
            mucopy(d).wait_recv()
        total = mbuf[0]
        for i in range(1, N):
            total = total + mbuf[i]
        scalar = WARMTH + coef * jnp.sum(total, axis=1, keepdims=True)
        racc[...] = jnp.zeros((T, U), F32)

        @pl.when(low)
        def _():
            racc[...] = W[at_row(r), U:]

        for d in range(R - 1):
            @pl.when(z <= lax.rem(r - d - 1 + R, R))
            def _():
                for i in range(per):
                    mcopy(d, 1, i).wait_recv()
                racc[...] += mrecv[d, 1]

        r_st[...] = r_st[...] + STEP * (coef * racc[...] - scalar * r_st[...])

        @pl.when(b == BLOCKS - 1)
        def _():
            r_full[at_row(r), :] = r_st[...]
            for d in range(R - 1):
                gcopy(d, 1).start()

        racc[...] = W[at_row(r), :U]
        for d in range(R - 1):
            for i in range(per):
                mcopy(d, 0, i).wait_recv()
            racc[...] += mrecv[d, 0]
        c_st[...] = c_st[...] + STEP * (coef * racc[...] - scalar * c_st[...])
        c_full[at_row(r), :] = c_st[...]
        for d in range(R - 1):
            gcopy(d, 0).start()

        for d in range(N - 1):
            mucopy(d).wait_send()
        for p in range(Z):
            @pl.when(jnp.logical_and(p <= z, z < Z - 1))
            def _():
                for s in range(2):
                    flow(p, 2, s).wait_send()

            @pl.when(jnp.logical_and(p >= z, z > 0))
            def _():
                for s in range(2):
                    flow(p, -2, s).wait_send()
        for d in range(R - 1):
            for s in range(2):
                inplane(d, rows[d], s).wait_send()
            for i in range(per):
                mcopy(d, 0, i).wait_send()

        @pl.when(low)
        def _():
            for d in range(R - 1):
                for i in range(per):
                    mcopy(d, 1, i).wait_send()

        @pl.when(z < r)
        def _():
            for i in range(per):
                upcopy(i, c + 2).wait_send()

        @pl.when(b == 0)
        def _():
            lo_out(2).wait()
            lo_out(3).wait()

        @pl.when(b < BLOCKS - 1)
        def _():
            greet(bar)

    for which in range(2):
        for d in range(R - 1):
            gcopy(d, which).wait()


def kernel_body(hist_corr, hist_resp, row_corr, row_resp):
    R, N = lax.axis_size("row"), lax.axis_size("col")
    Z = N // 2
    M, U = row_corr.shape
    S = hist_corr.shape[0]
    T = M // R
    per = U // CH
    coef = 1.0 / math.sqrt(S * R)
    dma, vmem = pltpu.SemaphoreType.DMA, pltpu.VMEM
    scratch = [
        vmem((S, U), BF16),
        vmem((S, U), BF16),
        vmem((S, U), F8),
        vmem((2, S // 4, U), F8),
        vmem((STAGES, PIECE, U), F32),
        vmem((T, U), F32),
        vmem((T, U), F32),
        vmem((T, U), F32),
        vmem((2 * M, U), BF16),
        vmem((2 * M, 2 * U), BF16),
        vmem((M, 2 * U), F32),
        vmem((M, U), F32),
        vmem((M, U), F32),
        vmem((M, U), F32),
        vmem((Z, T, U), F32),
        vmem((R - 1, 2, T, U), F32),
        vmem((N, T, 128), F32),
        pltpu.SemaphoreType.REGULAR,
        dma((3,)),
        dma((STAGES,)),
        dma((2,)),
        dma((2,)),
    ]
    scratch += [dma((per,))] * 4 + [dma((R - 1, 2, per))] * 2 + [dma((R - 1, 2))] * 2
    scratch += [dma((Z, 2))] * 4 + [dma((R - 1, 2))] * 2 + [dma((R,))] * 2 + [dma((N - 1,))] * 2
    hbm, whole = pl.BlockSpec(memory_space=pl.ANY), pl.BlockSpec(memory_space=pltpu.VMEM)
    full = jax.ShapeDtypeStruct((M, U), F32)
    out = pl.pallas_call(
        functools.partial(blocks_kernel, coef, R, Z),
        out_shape=[full, full, jax.ShapeDtypeStruct((S, U), F8)],
        in_specs=[hbm] * 4,
        out_specs=[whole, whole, hbm],
        scratch_shapes=scratch,
        name="blocks",
        compiler_params=pltpu.CompilerParams(collective_id=1, has_side_effects=True, vmem_limit_bytes=67_043_328),
    )(hist_corr, hist_resp, row_corr, row_resp)
    return tuple(out[:2])


def solution(mesh):
    R, N = mesh.shape["row"], mesh.shape["col"]
    body = kernel_body if N == 2 * R and R == 4 else plain_body
    in_specs = (P("row", "col"), P("row", "col"), P(None, "col"), P(None, "col"))
    out_specs = (P(None, "col"), P(None, "col"))
    return jax.shard_map(body, mesh=mesh, in_specs=in_specs, out_specs=out_specs, check_vma=False)
```

```python
import functools
import math

import jax
import jax.numpy as jnp
from jax import lax
from jax.experimental import pallas as pl
from jax.experimental.pallas import tpu as pltpu
from jax.sharding import PartitionSpec as P

BLOCKS = 4
STEP = 0.2
WARMTH = 0.6


def plain_body(hist_corr, hist_resp, row_corr, row_resp):
    rows = lax.axis_size("row")
    span = row_corr.shape[0] // rows
    coef = 1.0 / math.sqrt(hist_corr.shape[0] * rows)
    start = lax.axis_index("row") * span
    corr = lax.dynamic_slice_in_dim(row_corr, start, span, 0)
    resp = lax.dynamic_slice_in_dim(row_resp, start, span, 0)

    def dot(a, b, dims):
        return lax.dot_general(
            a, b, (dims, ((), ())), precision=lax.Precision.HIGH, preferred_element_type=jnp.float32
        )

    for _ in range(BLOCKS):
        energy = 3.0 * corr * resp
        slope = 1.5 * corr * corr
        mult = lax.psum(jnp.sum(energy * corr + slope * resp, axis=1), "col")
        full = lax.all_gather(corr, "row", axis=0, tiled=True)
        wide = lax.all_gather(energy, "col", axis=1, tiled=True)
        energy_rows = lax.all_to_all(wide, "row", split_axis=1, concat_axis=0, tiled=True)
        part_cross = dot(1.5 * full * full, hist_resp, ((1,), (1,)))
        turned = lax.all_to_all(part_cross, "row", split_axis=0, concat_axis=1, tiled=True)
        cross = lax.psum_scatter(turned, "col", scatter_dimension=1, tiled=True)
        part_corr = dot(energy_rows, hist_corr, ((1,), (0,)))
        part_resp = dot(energy_rows, hist_resp, ((1,), (0,)))
        mem_corr = lax.psum_scatter(part_corr, "row", scatter_dimension=0, tiled=True)
        mem_resp = lax.psum_scatter(part_resp, "row", scatter_dimension=0, tiled=True)
        scalar = WARMTH + coef * mult[:, None]
        next_corr = corr + STEP * (coef * (mem_corr + cross) - scalar * corr)
        resp = resp + STEP * (coef * mem_resp - scalar * resp)
        corr = next_corr
    return (
        lax.all_gather(corr, "row", axis=0, tiled=True),
        lax.all_gather(resp, "row", axis=0, tiled=True),
    )


MESH = pl.DeviceIdType.MESH
F32 = jnp.float32


BF16 = jnp.bfloat16
F8 = jnp.float8_e4m3fn
SCALE = 131072.0
STAGES = 4
PIECE = 128
CH = 512
KX = 1024
NN = (((1,), (0,)), ((), ()))
NT = (((1,), (1,)), ((), ()))


def split(x):
    hi = x.astype(BF16)
    return hi, (x - hi.astype(F32)).astype(BF16)


def dot(a, b, dims):
    return lax.dot_general(a, b, dims, preferred_element_type=F32)


def blocks_kernel(coef, R, Z, hc, hr, c0, r0, c_full, r_full, lo_hbm, *refs):
    refs = list(refs)
    take = lambda n: [refs.pop(0) for _ in range(n)]
    hchi, hrhi, hrlo, ring, stage = take(5)
    c_st, r_st, racc, dstack, estack, W = take(6)
    xown, xbuf, up, eall, mrecv, mbuf = take(6)
    bar, isem, ssem, lsem, osem = take(5)
    xs, xr, us, ur, ms, mrs, cs, crs = take(8)
    eus, eur, eds, edr, eis, eir, ps, pr, mus, mur = take(10)
    assert not refs
    T, U = c_st.shape
    H = T // 2
    M = R * T
    N = 2 * Z
    S = hc.shape[0]
    per = U // CH
    K = S // 4
    r, c = lax.axis_index("row"), lax.axis_index("col")
    z = lax.div(c, 2)
    k = c - 2 * z
    partner = 2 * z + 1 - k
    rows = [lax.rem(r + d, R) for d in range(1, R)]
    cols = [lax.rem(c + d, N) for d in range(1, N)]
    low = z <= r

    def rc(src, dst, ss, rs, row, col):
        return pltpu.make_async_remote_copy(
            src_ref=src, dst_ref=dst, send_sem=ss, recv_sem=rs, device_id=(row, col), device_id_type=MESH
        )

    def at_row(q):
        return pl.ds(pl.multiple_of(q * T, T), T)

    def half(h):
        return pl.ds(pl.multiple_of(h * U, U), U)

    def chunk(i, base=0):
        return pl.ds(base + i * CH, CH)

    pieces = S // PIECE
    group = CH // PIECE

    def x_row(t):
        side = jnp.where(lax.rem(t, 2) == 0, 1 - k, k)
        return side * U + lax.div(t, 2) * CH

    def piece_row(n):
        return pl.multiple_of(x_row(lax.div(n, group)) + lax.rem(n, group) * PIECE, PIECE)

    def piece_copy(src, start, n):
        slot = lax.rem(n, STAGES)
        return pltpu.make_async_copy(src.at[pl.ds(start, PIECE)], stage.at[slot], ssem.at[slot])

    def piece_start(n):
        @pl.when(n < pieces)
        def _():
            piece_copy(hr, piece_row(n), n).start()

        @pl.when(jnp.logical_and(n >= pieces, n < 2 * pieces))
        def _():
            piece_copy(hc, pl.multiple_of((n - pieces) * PIECE, PIECE), n).start()

    def piece_split(n, hi_ref, row, lo_ref, lo_row):
        slot = lax.rem(n, STAGES)
        piece_copy(hc, 0, n).wait()

        @pl.loop(0, PIECE // 32)
        def _(i):
            x = stage[slot, pl.ds(pl.multiple_of(i * 32, 32), 32), :]
            hi = x.astype(BF16)
            hi_ref[pl.ds(pl.multiple_of(row + i * 32, 32), 32), :] = hi
            lo_ref[pl.ds(pl.multiple_of(lo_row + i * 32, 32), 32), :] = ((x - hi.astype(F32)) * SCALE).astype(F8)

        piece_start(n + STAGES)

    for n in range(STAGES):
        piece_start(jnp.int32(n))
    inits = [
        pltpu.make_async_copy(c0, c_full, isem.at[0]),
        pltpu.make_async_copy(c0.at[at_row(r)], c_st, isem.at[1]),
        pltpu.make_async_copy(r0.at[at_row(r)], r_st, isem.at[2]),
    ]
    for cp in inits:
        cp.start()
    barrier = pltpu.get_barrier_semaphore()

    def greet(sem):
        for q in rows:
            pl.semaphore_signal(sem, inc=1, device_id=(q, c), device_id_type=MESH)
        for q in cols:
            pl.semaphore_signal(sem, inc=1, device_id=(r, q), device_id_type=MESH)

    greet(barrier)
    for cp in inits:
        cp.wait()
    pl.semaphore_wait(barrier, R - 1 + N - 1)

    def part(s):
        return pl.ds(s * H, H)

    def e_rows(q, s):
        return pl.ds(pl.multiple_of(q * T + s * H, H), H)

    def flow(p, step, s):
        ss, rs = (eus, eur) if step > 0 else (eds, edr)
        return rc(eall.at[p, part(s)], eall.at[p, part(s)], ss.at[p, s], rs.at[p, s], r, c + step)

    def inplane(d, p, s):
        return rc(eall.at[p, part(s)], W.at[e_rows(r, s), half(k)], eis.at[d, s], eir.at[d, s], p, c)

    def turn(p, s):
        @pl.when(p == r)
        def _():
            W[e_rows(r, s), half(k)] = eall[p, part(s)]

        @pl.when(p != r)
        def _():
            inplane(lax.rem(p - r + R, R) - 1, p, s).start()

    def pair(q):
        piece = W.at[at_row(q), half(k)]
        return rc(piece, piece, ps.at[q], pr.at[q], r, partner)

    def share(h):
        @pl.when(jnp.logical_or(z - r == h, r - z == h))
        def _():
            pair(r).start()
            for d in range(R - 1):
                for s in range(2):
                    inplane(d, rows[d], s).wait_recv()
                pair(lax.rem(r - d - 1 + R, R)).start()

    def hop(h, s):
        @pl.when(z - h >= 0)
        def _():
            flow(z - h, 2, s).wait_recv()

            @pl.when(z < Z - 1)
            def _():
                flow(z - h, 2, s).start()

        @pl.when(z + h <= Z - 1)
        def _():
            flow(z + h, -2, s).wait_recv()

            @pl.when(z > 0)
            def _():
                flow(z + h, -2, s).start()

            turn(z + h, s)

        @pl.when(z - h >= 0)
        def _():
            turn(z - h, s)

    def mucopy(d):
        return rc(mbuf.at[c], mbuf.at[c], mus.at[d], mur.at[d], r, cols[d])

    def xcopy(i):
        return rc(c_full.at[:, chunk(i)], xbuf.at[:, chunk(i)], xs.at[i], xr.at[i], r, partner)

    def upcopy(i, col):
        return rc(xown.at[:, chunk(i)], up.at[:, chunk(i)], us.at[i], ur.at[i], r, col)

    def mcopy(d, which, i):
        q = rows[d]
        return rc(
            W.at[at_row(q), chunk(i, which * U)],
            mrecv.at[d, which, :, chunk(i)],
            ms.at[d, which, i],
            mrs.at[d, which, i],
            q,
            c,
        )

    def gcopy(d, which):
        src, dst = (c_st, c_full) if which == 0 else (r_st, r_full)
        return rc(src, dst.at[at_row(r)], cs.at[d, which], crs.at[d, which], rows[d], c)

    def climb(zz, i):
        @pl.when(jnp.logical_and(z == zz, low))
        def _():
            xcopy(i).wait()
            both = xown[:, chunk(i)] + xbuf[:, chunk(i)]
            if zz > 0:
                upcopy(i, c).wait_recv()
                both = both + up[:, chunk(i)]
            xown[:, chunk(i)] = both
            if zz < Z - 1:
                @pl.when(z < r)
                def _():
                    upcopy(i, c + 2).start()

    def stack(dst_ref, i, x):
        hi, lo = split(x)
        dst_ref[pl.ds(pl.multiple_of(i * 32, 32), 32), :] = hi
        dst_ref[pl.ds(pl.multiple_of(M + i * 32, 32), 32), :] = lo

    def e_ready():
        share(Z - 1)
        for q in range(R):
            pair(q).wait()

        @pl.loop(0, M // 32)
        def _(i):
            stack(estack, i, W[pl.ds(pl.multiple_of(i * 32, 32), 32), :])

    def x_tile(b, t):
        @pl.when(b == 0)
        def _():
            @pl.loop(0, group)
            def _(g):
                n = t * group + g
                row = piece_row(n)
                piece_split(n, hrhi, row, hrlo, row)

        @pl.when(low)
        def _():
            out = c_full if t % 2 == 0 else xown
            where = chunk(t // 2)
            start = pl.multiple_of(x_row(jnp.int32(t)), CH)
            out[:, where] = jnp.zeros((M, CH), F32)

            @pl.loop(0, U // KX)
            def _(j):
                at = pl.ds(pl.multiple_of(j * KX, KX), KX)
                both = dstack[:, at]
                p = dot(both, hrhi[pl.ds(start, CH), at], NT)
                q = dot(both[:M], hrlo[pl.ds(start, CH), at].astype(BF16), NT)
                out[:, where] += p[:M] + p[M:] + q * (1.0 / SCALE)

            if t % 2 == 0:
                xcopy(t // 2).start()

    def resp_tile(i):
        @pl.when(low)
        def _():
            where = chunk(i, U)
            W[:, where] = jnp.zeros((M, CH), F32)

            @pl.loop(0, S // K)
            def _(j):
                at = pl.ds(pl.multiple_of(j * K, K), K)
                both = estack[:, at]
                p = dot(both, hrhi[at, chunk(i)], NN)
                q = dot(both[:M], hrlo[at, chunk(i)].astype(BF16), NN)
                W[:, where] += p[:M] + p[M:] + q * (1.0 / SCALE)

            for d in range(R - 1):
                mcopy(d, 1, i).start()

    def lo_in(j):
        return pltpu.make_async_copy(lo_hbm.at[pl.ds(j * K, K)], ring.at[j % 2], lsem.at[j % 2])

    def lo_out(j):
        return pltpu.make_async_copy(ring.at[j % 2], lo_hbm.at[pl.ds(j * K, K)], osem.at[j % 2])

    def corr_part(b, j):
        @pl.when(b == 0)
        def _():
            if j >= 2:
                lo_out(j - 2).wait()

            @pl.loop(0, K // PIECE)
            def _(g):
                n = pieces + j * (K // PIECE) + g
                piece_split(n, hchi, j * K + g * PIECE, ring.at[j % 2], g * PIECE)

            lo_out(j).start()

        @pl.when(b > 0)
        def _():
            lo_in(j).wait()

        @pl.loop(0, per)
        def _(i):
            at = pl.ds(pl.multiple_of(i * CH, CH), CH)
            both = estack[:, j * K : (j + 1) * K]
            p = dot(both, hchi[j * K : (j + 1) * K, at], NN)
            q = dot(both[:M], ring[j % 2, :, at].astype(BF16), NN)
            out = p[:M] + p[M:] + q * (1.0 / SCALE)
            if j == 0:
                W[:, at] = out
            else:
                W[:, at] += out

        if j < 2:
            @pl.when(b > 0)
            def _():
                lo_in(j + 2).start()

    @pl.loop(0, BLOCKS)
    def _(b):
        energy = 3.0 * c_st[...] * r_st[...]
        eall[z] = energy
        terms = energy * c_st[...] + 1.5 * c_st[...] * c_st[...] * r_st[...]
        part = terms[:, :128]
        for i in range(1, U // 128):
            part = part + terms[:, i * 128 : (i + 1) * 128]
        mbuf[c] = part

        @pl.when(b > 0)
        def _():
            lo_in(0).start()
            lo_in(1).start()
            pl.semaphore_wait(bar, R - 1 + N - 1)

        for s in range(2):
            @pl.when(z < Z - 1)
            def _():
                flow(z, 2, s).start()

            @pl.when(z > 0)
            def _():
                flow(z, -2, s).start()

        for s in range(2):
            turn(z, s)
        for d in range(N - 1):
            mucopy(d).start()
        hop(1, 0)
        hop(1, 1)
        hop(2, 0)
        hop(2, 1)

        @pl.when(b > 0)
        def _():
            for d in range(R - 1):
                gcopy(d, 0).wait()

        hop(3, 0)

        @pl.loop(0, M // 32)
        def _(i):
            old = c_full[pl.ds(pl.multiple_of(i * 32, 32), 32), :]
            stack(dstack, i, 1.5 * old * old)

        hooks = {}

        def hook(n, f, *args):
            hooks.setdefault(n, []).append((f, args))

        for i in range(per):
            hook(min(2 * i + 2, 7), climb, 0, i)
        hook(0, hop, 3, 1)
        hook(3, share, 0)
        hook(5, share, 1)
        hook(6, share, 2)
        hook(7, climb, 1, 0)
        hook(7, e_ready)
        for n, zz, i in [(8, 1, 1), (9, 2, 0), (11, 1, 2), (11, 2, 1), (12, 3, 0), (14, 1, 3), (14, 2, 2)]:
            hook(n, climb, zz, i)
        for n in range(16):
            if n < 8:
                x_tile(b, n)
            elif n < 12:
                resp_tile(n - 8)
            else:
                corr_part(b, n - 12)
            for f, args in hooks.get(n, ()):
                f(*args)

        for i in range(per):
            if i == per - 1:
                climb(Z - 2, i)
            if i >= 1:
                climb(Z - 1, i)

            @pl.when(z == r)
            def _():
                W[:, chunk(i)] += xown[:, chunk(i)]

            for d in range(R - 1):
                mcopy(d, 0, i).start()

        for d in range(N - 1):
            mucopy(d).wait_recv()
        total = mbuf[0]
        for i in range(1, N):
            total = total + mbuf[i]
        scalar = WARMTH + coef * jnp.sum(total, axis=1, keepdims=True)
        racc[...] = jnp.zeros((T, U), F32)

        @pl.when(low)
        def _():
            racc[...] = W[at_row(r), U:]

        for d in range(R - 1):
            @pl.when(z <= lax.rem(r - d - 1 + R, R))
            def _():
                for i in range(per):
                    mcopy(d, 1, i).wait_recv()
                racc[...] += mrecv[d, 1]

        r_st[...] = r_st[...] + STEP * (coef * racc[...] - scalar * r_st[...])

        @pl.when(b == BLOCKS - 1)
        def _():
            r_full[at_row(r), :] = r_st[...]
            for d in range(R - 1):
                gcopy(d, 1).start()

        racc[...] = W[at_row(r), :U]
        for d in range(R - 1):
            for i in range(per):
                mcopy(d, 0, i).wait_recv()
            racc[...] += mrecv[d, 0]
        c_st[...] = c_st[...] + STEP * (coef * racc[...] - scalar * c_st[...])
        c_full[at_row(r), :] = c_st[...]
        for d in range(R - 1):
            gcopy(d, 0).start()

        for d in range(N - 1):
            mucopy(d).wait_send()
        for p in range(Z):
            @pl.when(jnp.logical_and(p <= z, z < Z - 1))
            def _():
                for s in range(2):
                    flow(p, 2, s).wait_send()

            @pl.when(jnp.logical_and(p >= z, z > 0))
            def _():
                for s in range(2):
                    flow(p, -2, s).wait_send()
        for d in range(R - 1):
            for s in range(2):
                inplane(d, rows[d], s).wait_send()
            for i in range(per):
                mcopy(d, 0, i).wait_send()

        @pl.when(low)
        def _():
            for d in range(R - 1):
                for i in range(per):
                    mcopy(d, 1, i).wait_send()

        @pl.when(z < r)
        def _():
            for i in range(per):
                upcopy(i, c + 2).wait_send()

        @pl.when(b == 0)
        def _():
            lo_out(2).wait()
            lo_out(3).wait()

        @pl.when(b < BLOCKS - 1)
        def _():
            greet(bar)

    for which in range(2):
        for d in range(R - 1):
            gcopy(d, which).wait()


def kernel_body(hist_corr, hist_resp, row_corr, row_resp):
    R, N = lax.axis_size("row"), lax.axis_size("col")
    Z = N // 2
    M, U = row_corr.shape
    S = hist_corr.shape[0]
    T = M // R
    per = U // CH
    coef = 1.0 / math.sqrt(S * R)
    dma, vmem = pltpu.SemaphoreType.DMA, pltpu.VMEM
    scratch = [
        vmem((S, U), BF16),
        vmem((S, U), BF16),
        vmem((S, U), F8),
        vmem((2, S // 4, U), F8),
        vmem((STAGES, PIECE, U), F32),
        vmem((T, U), F32),
        vmem((T, U), F32),
        vmem((T, U), F32),
        vmem((2 * M, U), BF16),
        vmem((2 * M, 2 * U), BF16),
        vmem((M, 2 * U), F32),
        vmem((M, U), F32),
        vmem((M, U), F32),
        vmem((M, U), F32),
        vmem((Z, T, U), F32),
        vmem((R - 1, 2, T, U), F32),
        vmem((N, T, 128), F32),
        pltpu.SemaphoreType.REGULAR,
        dma((3,)),
        dma((STAGES,)),
        dma((2,)),
        dma((2,)),
    ]
    scratch += [dma((per,))] * 4 + [dma((R - 1, 2, per))] * 2 + [dma((R - 1, 2))] * 2
    scratch += [dma((Z, 2))] * 4 + [dma((R - 1, 2))] * 2 + [dma((R,))] * 2 + [dma((N - 1,))] * 2
    hbm, whole = pl.BlockSpec(memory_space=pl.ANY), pl.BlockSpec(memory_space=pltpu.VMEM)
    full = jax.ShapeDtypeStruct((M, U), F32)
    out = pl.pallas_call(
        functools.partial(blocks_kernel, coef, R, Z),
        out_shape=[full, full, jax.ShapeDtypeStruct((S, U), F8)],
        in_specs=[hbm] * 4,
        out_specs=[whole, whole, hbm],
        scratch_shapes=scratch,
        name="blocks",
        compiler_params=pltpu.CompilerParams(collective_id=1, has_side_effects=True, vmem_limit_bytes=67_043_328),
    )(hist_corr, hist_resp, row_corr, row_resp)
    return tuple(out[:2])


def solution(mesh):
    R, N = mesh.shape["row"], mesh.shape["col"]
    body = kernel_body if N == 2 * R and R == 4 else plain_body
    in_specs = (P("row", "col"), P("row", "col"), P(None, "col"), P(None, "col"))
    out_specs = (P(None, "col"), P(None, "col"))
    return jax.shard_map(body, mesh=mesh, in_specs=in_specs, out_specs=out_specs, check_vma=False)
```
